32 devices in a mesh: ax: 4 (over y, x), az: 8 (over z, core).
Axes of the slice: x: 2, y: 2, z: 4, core: 2. Of those that a mesh axis runs over, the one named last changes fastest.
Arguments:
- velocity: float32 [3, 64, 512, 512], P(None, 'ax', 'az'), may hold values from -6 to 6
- viscosity: float32 [64, 512, 512], P('ax', 'az'), may hold values from 0.5 to 4
- force: float32 [3, 8192, 512], P(None, ('ax', 'az')), may hold values from -6 to 6
- area: float32 [8192], P(('ax', 'az')), may hold values from 0.5 to 2
- adjacency: int32 [8192, 4], P(('ax', 'az')), may hold values from 0 to 8191, as said below
- crossing: int32 [8192, 1], P(('ax', 'az')), may hold values from 0 to 31; in each aligned block of 256 rows (0 to 255, 256 to 511, ...) at most 16 rows name the same one
- cell: int32 [8192], P(('ax', 'az')), may hold values from 0 to 1023
Outputs:
- updated: float32 [3, 64, 512, 512], P(None, 'ax', 'az')
The draws below stay inside these ranges and needn't reach their ends.
Inputs may be any that keep to these rules, and one draw needn't show every extreme that they name: adjacency[p, k] differs from p by at most 32; the first neighbour of a panel lies exactly 32 away unless the surface ends there. `crossing`: among the panels of one device no brick is crossed by more than 16 panels, a bound that some block reaches.
All inputs are finite; a program needn't handle non-finite values.
Results may differ from the reference program's by a relative error of at most 0.000062.
Values sent between devices are 32-bit elements; how exact they have to be, the bound alone decides.
A program may use at most 128 MiB of HBM per device.

```python
import math
import jax
import jax.numpy as jnp
import numpy as np

CA = 16
CT = 64
CR = 512
PAN_DEV = 256
HALO = 32
BRICKS = 32
CAP = 16
PANELS = 8192
NA = 64
NT = 512
N_AZ = 8


def draw_adjacency(key, part):
    first_key = jax.random.fold_in(key, 11)
    rest_key = jax.random.fold_in(key, 12)
    index = jnp.arange(PANELS, dtype=jnp.int32)[:, None]
    sign = jax.random.randint(first_key, (PANELS, 1), 0, 2).astype(jnp.int32) * 2 - 1
    first = index + sign * HALO
    rest = index + jax.random.randint(rest_key, (PANELS, 3), -HALO, HALO + 1).astype(jnp.int32)
    joined = jnp.concatenate([first, rest], axis=1)
    return jnp.clip(joined, 0, PANELS - 1).astype(jnp.int32)


def plant(values, own_key, low, high):
    longest = values.shape.index(max(values.shape))
    spots = []
    for shift in (0, 1):
        where = [jax.random.randint(jax.random.fold_in(own_key, axis), (), 0, length) for axis, length in enumerate(values.shape)]
        where[longest] = (where[longest] + shift) % values.shape[longest]
        spots.append(tuple(where))
    return values.at[spots[0]].set(low).at[spots[1]].set(high)


def block_levels(stream_key, dims, shards, least, high):
    level = 1.0
    for position, shards_of in shards:
        draws = jax.random.uniform(jax.random.fold_in(jax.random.fold_in(stream_key, 6), position), (shards_of,), jnp.float32, least / len(shards), high / len(shards))
        level = level * jnp.repeat(jnp.exp(draws), dims[position] // shards_of).reshape((-1,) + (1,) * (len(dims) - 1 - position))
    return level


def routed_block(stream_key, own, number, rows, number_of, top, most, skew):
    order = jax.random.permutation(stream_key, number_of)
    crowded, common = portions_of(number_of, rows * top, most, skew, True), portions_of(number_of, rows * top, most, skew, False)
    places = jnp.arange(number_of)

    def named(sizes, offset_by):
        used = int((sizes > 0).sum())
        fixed = max(1, used // 4)
        shifted = fixed + (places - fixed + offset_by * (used - fixed)) % max(1, number_of - fixed)
        return jnp.zeros((number_of,), jnp.int32).at[order[jnp.where(places < fixed, places, shifted)]].set(jnp.asarray(sizes, jnp.int32))

    sizes = jnp.where(number % 4 == 0, named(crowded, number // 4), named(common, number - number // 4 - 1))
    mixed = jax.random.permutation(jax.random.fold_in(own, 3), number_of)
    giver, taker = mixed[0:number_of // 2 * 2:2], mixed[1:number_of // 2 * 2:2]
    slack = jnp.minimum(sizes[giver] - 1, most - sizes[taker]) // 2
    slack = jnp.where((giver == order[0]) | (taker == order[0]) | (sizes[taker] == 0), 0, jnp.maximum(slack, 0))
    shifted = jax.random.randint(jax.random.fold_in(own, 4), (number_of // 2,), 0, 1 << 20) % (slack + 1)
    sizes = sizes.at[giver].add(-shifted).at[taker].add(shifted)
    members = jnp.searchsorted(jnp.cumsum(sizes), jnp.arange(rows * top), side="right").astype(jnp.int32)
    grid = members.reshape(top, rows).T
    grid = grid[jax.random.permutation(jax.random.fold_in(own, 1), rows)]
    offset_by = jax.random.randint(jax.random.fold_in(own, 2), (rows, 1), 0, top)
    return jnp.take_along_axis(grid, (jnp.arange(top)[None, :] + offset_by) % top, axis=1)


def portions_of(count, total, limit, lean, full):
    portions = [(1 << 20) // math.isqrt(rank ** lean) + 1 for rank in range(1, count + 1)]
    largest = limit if full else min(limit, max(-(-total // count), total * portions[0] // sum(portions)))
    least = 1 if total - largest >= count - 1 else 0
    given, surplus = [largest] + [least] * (count - 1), total - largest - least * (count - 1)
    while surplus > 0:
        candidates = [i for i in range(1, count) if given[i] < largest] or [i for i in range(1, count) if given[i] < limit]
        whole, budget = sum([portions[i] for i in candidates]), surplus
        for i in candidates:
            more = min(limit - given[i], max(1, budget * portions[i] // whole), surplus)
            given[i] = given[i] + more
            surplus = surplus - more
    return np.array(given)


def noise(own_key, dims, deviation, bound, split=(), kind=jnp.bfloat16):
    values = deviation * jax.random.normal(own_key, dims, jnp.float32)
    if split:
        values = values * block_levels(own_key, dims, split, -0.22, 0.18)
    return jnp.clip(values, -bound, bound).astype(kind)


def setup_inputs(seed: int = 0) -> dict:
    arg_keys = jax.random.split(jax.random.key(seed), 8)
    velocity = noise(arg_keys[0], (3, NA, NT, CR), 1.0, 6.0, ((1, 4), (2, 8)), jnp.float32)
    viscosity = jnp.clip(jnp.exp(math.log(4.0) - 2.0794415 * jax.random.uniform(arg_keys[1], (NA, NT, CR), jnp.float32) ** block_levels(arg_keys[1], (NA, NT, CR), ((0, 4), (1, 8)), -0.2, 0.2)), 0.5, 4.0)
    force = noise(arg_keys[2], (3, PANELS, CR), 1.0, 6.0, ((1, 32),), jnp.float32)
    area = jnp.clip(jnp.exp(math.log(2.0) - 1.3862944 * jax.random.uniform(arg_keys[3], (PANELS,), jnp.float32) ** block_levels(arg_keys[3], (PANELS,), ((0, 32),), -0.2, 0.2)), 0.5, 2.0)
    adjacency = draw_adjacency(jax.random.fold_in(arg_keys[7], 71), 0)
    crossing_keys = jax.random.split(jax.random.fold_in(arg_keys[5], 1), PANELS // PAN_DEV)
    crossing_turns = jax.random.permutation(jax.random.fold_in(arg_keys[5], 3), PANELS // PAN_DEV)
    crossing = jax.vmap(lambda own, number: routed_block(jax.random.fold_in(arg_keys[5], 2), own, number, PAN_DEV, BRICKS, 1, CAP, 2))(crossing_keys, crossing_turns).reshape((PANELS, 1))
    cell = plant(jax.random.randint(arg_keys[6], (PANELS,), 0, CA * CT), jax.random.fold_in(arg_keys[6], 1), 0, (CA * CT) - 1).astype(jnp.int32)
    return {"velocity": velocity, "viscosity": viscosity, "force": force, "area": area, "adjacency": adjacency, "crossing": crossing, "cell": cell}


step_size = 0.1
coupling = 0.2


def face_term(mu, mu_other, field, field_other):
    return 0.5 * (mu + mu_other)[None] * (field_other - field)


def viscous_sum(field, mu):
    fpad = jnp.pad(field, ((0, 0), (1, 1), (0, 0), (0, 0)))
    mpad = jnp.pad(mu, ((1, 1), (0, 0), (0, 0)))
    total = face_term(mu, mpad[2:], field, fpad[:, 2:])
    total = total + face_term(mu, mpad[:-2], field, fpad[:, :-2])
    total = total + face_term(mu, jnp.roll(mu, -1, axis=1), field, jnp.roll(field, -1, axis=2))
    total = total + face_term(mu, jnp.roll(mu, 1, axis=1), field, jnp.roll(field, 1, axis=2))
    fpad = jnp.pad(field, ((0, 0), (0, 0), (0, 0), (1, 1)))
    mpad = jnp.pad(mu, ((0, 0), (0, 0), (1, 1)))
    total = total + face_term(mu, mpad[:, :, 2:], field, fpad[:, :, :, 2:])
    total = total + face_term(mu, mpad[:, :, :-2], field, fpad[:, :, :, :-2])
    return total


def reference(velocity, viscosity, force, area, adjacency, crossing, cell):
    neighbours = jnp.take(force, adjacency, axis=1)
    jump = area[None, :, None] * (force + coupling * jnp.sum(neighbours - force[:, :, None, :], axis=2))
    dest = crossing[:, 0]
    brick_ax = dest // N_AZ
    brick_az = dest % N_AZ
    row = (brick_ax * CA + cell // CT) * NT + brick_az * CT + cell % CT
    tiles = jnp.transpose(jump, (1, 0, 2)).reshape(PANELS, 3 * CR)
    deposit = jax.ops.segment_sum(tiles, row.astype(jnp.int32), num_segments=NA * NT)
    deposit = jnp.transpose(deposit.reshape(NA, NT, 3, CR), (2, 0, 1, 3))
    viscous = viscous_sum(velocity, viscosity)
    return velocity + step_size * viscous + deposit
```

```python
import functools

import jax
import jax.numpy as jnp
from jax import lax
from jax.experimental import pallas as pl
from jax.experimental.pallas import tpu as pltpu
from jax.sharding import PartitionSpec as P

HALO = 32
LANES = 128

step_size = 0.1
coupling = 0.2


def split(x):
    hi = x.astype(jnp.bfloat16)
    lo = (x - hi.astype(jnp.float32)).astype(jnp.bfloat16)
    return hi, lo


def dot(a, b):
    return jnp.dot(a, b, preferred_element_type=jnp.float32)


def exchange(n_ax, n_az, cap, vel, visc, force, rows, cols, base, got, gcell,
             velx, viscx, ext, send, scell, edges, edge_in, outbuf,
             load_sem, halo_send, halo_recv, tile_send, tile_recv,
             cell_send, cell_recv, own_sem, out_sem):
    n = n_ax * n_az
    ax, az = lax.axis_index("ax"), lax.axis_index("az")
    me = ax * n_az + az
    ncomp, na, nt, nr = vel.shape
    pan = force.shape[1]
    slots = n * cap

    def place(linear):
        return (linear // n_az, lax.rem(linear, n_az))

    def remote(src, dst, ssem, rsem, device):
        return pltpu.make_async_remote_copy(
            src_ref=src, dst_ref=dst, send_sem=ssem, recv_sem=rsem,
            device_id=device, device_id_type=pl.DeviceIdType.MESH)

    loads = [
        pltpu.make_async_copy(force, ext.at[:, pl.ds(HALO, pan)], load_sem.at[0]),
        pltpu.make_async_copy(vel, velx.at[:, pl.ds(1, na)], load_sem.at[1]),
        pltpu.make_async_copy(visc, viscx.at[pl.ds(1, na)], load_sem.at[2]),
    ]
    for c in loads:
        c.start()

    barrier = pltpu.get_barrier_semaphore()

    def greet(k, carry):
        pl.semaphore_signal(barrier, inc=1, device_id=place(lax.rem(me + k, n)),
                            device_id_type=pl.DeviceIdType.MESH)
        return carry

    lax.fori_loop(1, n, greet, 0)
    pl.semaphore_wait(barrier, n - 1)

    up, down = place(lax.rem(me + 1, n)), place(lax.rem(me + n - 1, n))
    ax_up, ax_down = lax.rem(ax + 1, n_ax), lax.rem(ax + n_ax - 1, n_ax)
    az_up, az_down = lax.rem(az + 1, n_az), lax.rem(az + n_az - 1, n_az)

    def halo(i, src, dst, device):
        return remote(src, dst, halo_send.at[i], halo_recv.at[i], device)

    fhalo = [
        halo(0, force.at[:, pl.ds(pan - HALO, HALO)], ext.at[:, pl.ds(0, HALO)], up),
        halo(1, force.at[:, pl.ds(0, HALO)], ext.at[:, pl.ds(HALO + pan, HALO)], down),
    ]
    for c in fhalo:
        c.start()
    ahalo = [
        halo(2, vel.at[:, na - 1], velx.at[:, 0], (ax_up, az)),
        halo(3, vel.at[:, 0], velx.at[:, na + 1], (ax_down, az)),
        halo(4, visc.at[na - 1], viscx.at[0], (ax_up, az)),
        halo(5, visc.at[0], viscx.at[na + 1], (ax_down, az)),
    ]

    dest_row, cell_col = rows[0:1, :], cols[:, 1:2]
    dest_col = cols[:, 0:1]
    same = dest_col == dest_row
    r0 = lax.broadcasted_iota(jnp.int32, (pan, pan), 0)
    r1 = lax.broadcasted_iota(jnp.int32, (pan, pan), 1)
    rank_row = jnp.sum((same & (r0 < r1)).astype(jnp.float32), axis=0, keepdims=True)
    rank_col = jnp.sum((same & (r1 < r0)).astype(jnp.float32), axis=1, keepdims=True)
    target = (dest_row * cap + rank_row).astype(jnp.int32)
    hits = lax.broadcasted_iota(jnp.int32, (slots, pan), 0) == target
    scale = jnp.sum(jnp.where(hits, coupling * rows[2:3, :], 0.0), axis=1, keepdims=True)
    q = lax.broadcasted_iota(jnp.int32, (pan, pan + 2 * HALO), 1).astype(jnp.float32)
    p = lax.broadcasted_iota(jnp.int32, (pan, pan + 2 * HALO), 0).astype(jnp.float32)
    count = (q == p + HALO).astype(jnp.float32)
    for k in range(4):
        count = count + (q == cols[:, 3 + k:4 + k]).astype(jnp.float32)
    pick = dot(hits.astype(jnp.float32).astype(jnp.bfloat16), count.astype(jnp.bfloat16))
    pick = pick.astype(jnp.bfloat16)

    big = jnp.floor((cell_col + 1.0) * (1.0 / 64.0))
    small = (cell_col + 1.0) - 64.0 * big
    lane = lax.broadcasted_iota(jnp.int32, (pan, LANES), 1).astype(jnp.float32)
    at_rank = lane == rank_col
    owner = (lax.broadcasted_iota(jnp.int32, (n, pan), 0).astype(jnp.float32) == dest_row)
    owner = owner.astype(jnp.float32).astype(jnp.bfloat16)
    cells = (64.0 * dot(owner, jnp.where(at_rank, big, 0.0).astype(jnp.bfloat16))
             + dot(owner, jnp.where(at_rank, small, 0.0).astype(jnp.bfloat16)) - 1.0)
    for d in range(n):
        scell[d] = cells[d:d + 1, :]

    loads[0].wait()
    for c in fhalo:
        c.wait()
    for c in range(ncomp):
        hi, lo = split(ext[c])
        tile = (dot(pick, hi) + dot(pick, lo)) * scale
        send[:, :, c * nr:(c + 1) * nr] = tile.reshape(n, cap, nr)

    def tiles_to(k):
        d = lax.rem(me + k, n)
        return (remote(send.at[d], got.at[me], tile_send.at[k], tile_recv.at[k], place(d)),
                remote(scell.at[d], gcell.at[me], cell_send.at[k], cell_recv.at[k], place(d)))

    for c in ahalo:
        c.start()
    loads[1].wait()
    loads[2].wait()
    for c in range(ncomp):
        edges[0, c] = velx[c, 1:na + 1, 0, :]
        edges[1, c] = velx[c, 1:na + 1, nt - 1, :]
    edges[0, ncomp] = viscx[1:na + 1, 0, :]
    edges[1, ncomp] = viscx[1:na + 1, nt - 1, :]
    zhalo = [
        halo(6, edges.at[1], edge_in.at[0], (ax, az_up)),
        halo(7, edges.at[0], edge_in.at[1], (ax, az_down)),
    ]
    for c in zhalo:
        c.start()

    def start_tiles(k, carry):
        a, b = tiles_to(k)
        a.start()
        b.start()
        return carry

    lax.fori_loop(1, n, start_tiles, 0)
    own = [pltpu.make_async_copy(send.at[me], got.at[me], own_sem.at[0]),
           pltpu.make_async_copy(scell.at[me], gcell.at[me], own_sem.at[1])]
    for c in own:
        c.start()

    for c in ahalo + zhalo:
        c.wait()

    @pl.when(ax == 0)
    def _():
        velx[:, 0] = jnp.zeros((ncomp, nt, nr), jnp.float32)
        viscx[0] = jnp.zeros((nt, nr), jnp.float32)

    @pl.when(ax == n_ax - 1)
    def _():
        velx[:, na + 1] = jnp.zeros((ncomp, nt, nr), jnp.float32)
        viscx[na + 1] = jnp.zeros((nt, nr), jnp.float32)

    row_id = lax.broadcasted_iota(jnp.int32, (nt, nr), 0)
    lane_id = lax.broadcasted_iota(jnp.int32, (nt, nr), 1)

    def neighbours(x, low, high):
        left = jnp.where(row_id == 0, low, pltpu.roll(x, 1, 0))
        right = jnp.where(row_id == nt - 1, high, pltpu.roll(x, nt - 1, 0))
        inner = jnp.where(lane_id == 0, 0.0, pltpu.roll(x, 1, 1))
        outer = jnp.where(lane_id == nr - 1, 0.0, pltpu.roll(x, nr - 1, 1))
        return left, right, inner, outer

    def stored(i, slot):
        return pltpu.make_async_copy(outbuf.at[slot], base.at[:, i], out_sem.at[slot])

    def plane(i, slot, first):
        if not first:
            stored(i - 2, slot).wait()
        mu = viscx[i + 1]
        sides = neighbours(mu, edge_in[0, ncomp, pl.ds(i, 1), :], edge_in[1, ncomp, pl.ds(i, 1), :])
        faces = [mu + s for s in (viscx[i], viscx[i + 2]) + sides]
        for c in range(ncomp):
            f = velx[c, i + 1]
            near = neighbours(f, edge_in[0, c, pl.ds(i, 1), :], edge_in[1, c, pl.ds(i, 1), :])
            near = (velx[c, i], velx[c, i + 2]) + near
            total = faces[0] * (near[0] - f)
            for w, g in zip(faces[1:], near[1:]):
                total = total + w * (g - f)
            outbuf[slot, c] = f + (0.5 * step_size) * total
        stored(i, slot).start()

    plane(0, 0, True)
    plane(1, 1, True)

    def planes(j, carry):
        plane(2 * j, 0, False)
        plane(2 * j + 1, 1, False)
        return carry

    lax.fori_loop(1, na // 2, planes, 0)
    stored(na - 2, 0).wait()
    stored(na - 1, 1).wait()

    for c in own:
        c.wait()

    def finish_tiles(k, carry):
        a, b = tiles_to(k)
        a.wait()
        b.wait()
        return carry

    lax.fori_loop(1, n, finish_tiles, 0)


def settle(cap, base, got, gcell, out, hi, lo, crow):
    step = pl.program_id(0)
    ncomp, blk, nt, nr = base.shape
    slots = got.shape[0]
    n = slots // cap

    @pl.when(step == 0)
    def _():
        cells = gcell[...].reshape(n, LANES)
        big = jnp.floor((cells + 1.0) * (1.0 / 64.0))
        small = (cells + 1.0) - 64.0 * big
        spread = (lax.broadcasted_iota(jnp.int32, (LANES, slots), 0)
                  == lax.rem(lax.broadcasted_iota(jnp.int32, (LANES, slots), 1), cap))
        spread = spread.astype(jnp.float32).astype(jnp.bfloat16)
        wide = 64.0 * dot(big.astype(jnp.bfloat16), spread) + dot(small.astype(jnp.bfloat16), spread)
        mine = (lax.broadcasted_iota(jnp.int32, (n, slots), 0)
                == lax.broadcasted_iota(jnp.int32, (n, slots), 1) // cap)
        crow[...] = jnp.sum(jnp.where(mine, wide, 0.0), axis=0, keepdims=True) - 1.0
        h, l = split(got[...])
        hi[...] = h
        lo[...] = l

    here = lax.broadcasted_iota(jnp.int32, (blk * nt, slots), 0) + step * (blk * nt)
    landing = (crow[...].astype(jnp.int32) == here).astype(jnp.float32).astype(jnp.bfloat16)
    for c in range(ncomp):
        cs = slice(c * nr, (c + 1) * nr)
        deposit = dot(landing, hi[:, cs]) + dot(landing, lo[:, cs])
        out[c] = base[c] + deposit.reshape(blk, nt, nr)


def on_device(n_ax, n_az, velocity, viscosity, force, area, adjacency, crossing, cell):
    n = n_ax * n_az
    ncomp, pan, nr = force.shape
    na, nt = velocity.shape[1:3]
    cap = max(2, 2 * pan // n)
    cap = -(-cap // 8) * 8
    f32 = jnp.float32
    first = lax.axis_index(("ax", "az")) * pan - HALO
    rows = jnp.concatenate([
        crossing.reshape(1, pan).astype(f32), cell.reshape(1, pan).astype(f32),
        area.reshape(1, pan), (adjacency - first).T.astype(f32), jnp.zeros((1, pan), f32)], axis=0)
    cols = rows.T
    any_ = pl.BlockSpec(memory_space=pl.ANY)
    vmem = pl.BlockSpec(memory_space=pltpu.VMEM)
    base, got, gcell = pl.pallas_call(
        functools.partial(exchange, n_ax, n_az, cap),
        out_shape=(jax.ShapeDtypeStruct(velocity.shape, f32),
                   jax.ShapeDtypeStruct((n, cap, ncomp * nr), f32),
                   jax.ShapeDtypeStruct((n, 1, LANES), f32)),
        in_specs=[any_, any_, any_, vmem, vmem],
        out_specs=(any_, any_, any_),
        scratch_shapes=[
            pltpu.VMEM((ncomp, na + 2, nt, nr), f32),
            pltpu.VMEM((na + 2, nt, nr), f32),
            pltpu.VMEM((ncomp, pan + 2 * HALO, nr), f32),
            pltpu.VMEM((n, cap, ncomp * nr), f32),
            pltpu.VMEM((n, 1, LANES), f32),
            pltpu.VMEM((2, ncomp + 1, na, nr), f32),
            pltpu.VMEM((2, ncomp + 1, na, nr), f32),
            pltpu.VMEM((2, ncomp, nt, nr), f32),
            pltpu.SemaphoreType.DMA((3,)),
            pltpu.SemaphoreType.DMA((8,)),
            pltpu.SemaphoreType.DMA((8,)),
            pltpu.SemaphoreType.DMA((n,)),
            pltpu.SemaphoreType.DMA((n,)),
            pltpu.SemaphoreType.DMA((n,)),
            pltpu.SemaphoreType.DMA((n,)),
            pltpu.SemaphoreType.DMA((2,)),
            pltpu.SemaphoreType.DMA((2,)),
        ],
        compiler_params=pltpu.CompilerParams(collective_id=0, has_side_effects=True),
        name="exchange",
    )(velocity, viscosity, force, rows, cols)
    slots = n * cap
    blk = max(1, 256 // nt)
    window = pl.BlockSpec((ncomp, blk, nt, nr), lambda s: (0, s, 0, 0))
    return pl.pallas_call(
        functools.partial(settle, cap),
        out_shape=jax.ShapeDtypeStruct(velocity.shape, f32),
        grid=(na // blk,),
        in_specs=[window,
                  pl.BlockSpec((slots, ncomp * nr), lambda s: (0, 0)),
                  pl.BlockSpec((n, 1, LANES), lambda s: (0, 0, 0))],
        out_specs=window,
        scratch_shapes=[pltpu.VMEM((slots, ncomp * nr), jnp.bfloat16),
                        pltpu.VMEM((slots, ncomp * nr), jnp.bfloat16),
                        pltpu.VMEM((1, slots), f32)],
        name="settle",
    )(base, got.reshape(slots, ncomp * nr), gcell)


def solution(mesh):
    n_ax, n_az = mesh.shape["ax"], mesh.shape["az"]
    in_specs = (
        P(None, "ax", "az", None),
        P("ax", "az", None),
        P(None, ("ax", "az"), None),
        P(("ax", "az")),
        P(("ax", "az"), None),
        P(("ax", "az"), None),
        P(("ax", "az")),
    )
    return jax.shard_map(
        functools.partial(on_device, n_ax, n_az), mesh=mesh, in_specs=in_specs,
        out_specs=P(None, "ax", "az", None), check_vma=False)
```

```python
import functools

import jax
import jax.numpy as jnp
from jax import lax
from jax.experimental import pallas as pl
from jax.experimental.pallas import tpu as pltpu
from jax.sharding import PartitionSpec as P

HALO = 32
LANES = 128

step_size = 0.1
coupling = 0.2


def split(x):
    hi = x.astype(jnp.bfloat16)
    lo = (x - hi.astype(jnp.float32)).astype(jnp.bfloat16)
    return hi, lo


def dot(a, b):
    return jnp.dot(a, b, preferred_element_type=jnp.float32)


def wide_row(cells, cap):
    m = cells.shape[0]
    slots = m * cap
    big = jnp.floor((cells + 1.0) * (1.0 / 64.0))
    small = (cells + 1.0) - 64.0 * big
    spread = (lax.broadcasted_iota(jnp.int32, (LANES, slots), 0)
              == lax.rem(lax.broadcasted_iota(jnp.int32, (LANES, slots), 1), cap))
    spread = spread.astype(jnp.float32).astype(jnp.bfloat16)
    wide = 64.0 * dot(big.astype(jnp.bfloat16), spread) + dot(small.astype(jnp.bfloat16), spread)
    mine = (lax.broadcasted_iota(jnp.int32, (m, slots), 0)
            == lax.broadcasted_iota(jnp.int32, (m, slots), 1) // cap)
    return jnp.sum(jnp.where(mine, wide, 0.0), axis=0, keepdims=True) - 1.0


def landing_of(crow, first, count):
    here = lax.broadcasted_iota(jnp.int32, (count, crow.shape[1]), 0) + first
    return (crow.astype(jnp.int32) == here).astype(jnp.float32).astype(jnp.bfloat16)


def exchange(n_ax, n_az, cap, vel, visc, force, dest_i, cell_i, area, adj_i, base, got, gcell,
             velx, viscx, ext, exthi, extlo, send, scell, edges, edge_in, acc,
             tiles, tcell, thi, tlo,
             load_sem, halo_send, halo_recv, tile_send, tile_recv,
             cell_send, cell_recv, own_sem, out_sem):
    n, half_n = n_ax * n_az, n_az // 2
    early = n_ax // 2
    ax, az = lax.axis_index("ax"), lax.axis_index("az")
    me = ax * n_az + az
    half, spot = az // half_n, lax.rem(az, half_n)
    ncomp, na, nt, nr = vel.shape
    pan = force.shape[1]
    slots = n * cap
    f32, bf16 = jnp.float32, jnp.bfloat16

    def place(linear):
        return (linear // n_az, lax.rem(linear, n_az))

    def remote(src, dst, ssem, rsem, device):
        return pltpu.make_async_remote_copy(
            src_ref=src, dst_ref=dst, send_sem=ssem, recv_sem=rsem,
            device_id=device, device_id_type=pl.DeviceIdType.MESH)

    barrier = pltpu.get_barrier_semaphore()

    def greet(k, carry):
        pl.semaphore_signal(barrier, inc=1, device_id=place(lax.rem(me + k, n)),
                            device_id_type=pl.DeviceIdType.MESH)
        return carry

    lax.fori_loop(1, n, greet, 0)
    loads = [
        pltpu.make_async_copy(force, ext.at[:, pl.ds(HALO, pan)], load_sem.at[0]),
        pltpu.make_async_copy(vel, velx.at[:, pl.ds(1, na)], load_sem.at[1]),
        pltpu.make_async_copy(visc, viscx.at[pl.ds(1, na)], load_sem.at[2]),
    ]
    for c in loads:
        c.start()

    dest_row, cell_row = dest_i[...].astype(f32), cell_i[...].astype(f32)
    adj = (adj_i[...] - (me * pan - HALO)).astype(f32)
    rows = jnp.concatenate([dest_row, cell_row, adj, dest_row, dest_row], axis=0)
    cols = rows.T
    dest_col, cell_col = cols[:, 0:1], cols[:, 1:2]
    same = dest_col == dest_row
    r0 = lax.broadcasted_iota(jnp.int32, (pan, pan), 0)
    r1 = lax.broadcasted_iota(jnp.int32, (pan, pan), 1)
    rank_row = jnp.sum((same & (r0 < r1)).astype(f32), axis=0, keepdims=True)
    rank_col = jnp.sum((same & (r1 < r0)).astype(f32), axis=1, keepdims=True)
    dax = jnp.floor(dest_row * (1.0 / n_az))
    daz = dest_row - n_az * dax
    dhalf = jnp.floor(daz * (1.0 / half_n))
    turn = dax - ax.astype(f32)
    turn = jnp.where(turn < 0.0, turn + n_ax, turn)
    group = turn + jnp.where(dhalf == half.astype(f32), float(n_ax), 0.0)
    peer = group * half_n + (daz - half_n * dhalf)
    target = (peer * cap + rank_row).astype(jnp.int32)
    hits = lax.broadcasted_iota(jnp.int32, (slots, pan), 0) == target
    scale = jnp.sum(jnp.where(hits, coupling * area[...], 0.0), axis=1, keepdims=True)
    q = lax.broadcasted_iota(jnp.int32, (pan, pan + 2 * HALO), 1).astype(f32)
    p = lax.broadcasted_iota(jnp.int32, (pan, pan + 2 * HALO), 0).astype(f32)
    count = (q == p + HALO).astype(f32)
    for k in range(4):
        count = count + (q == cols[:, 2 + k:3 + k]).astype(f32)
    pick = dot(hits.astype(f32).astype(bf16), count.astype(bf16)).astype(bf16)

    pl.semaphore_wait(barrier, n - 1)

    up, down = place(lax.rem(me + 1, n)), place(lax.rem(me + n - 1, n))
    ax_up, ax_down = lax.rem(ax + 1, n_ax), lax.rem(ax + n_ax - 1, n_ax)
    az_up, az_down = lax.rem(az + 1, n_az), lax.rem(az + n_az - 1, n_az)

    def halo(i, src, dst, device):
        return remote(src, dst, halo_send.at[i], halo_recv.at[i], device)

    fhalo = [
        halo(0, force.at[:, pl.ds(pan - HALO, HALO)], ext.at[:, pl.ds(0, HALO)], up),
        halo(1, force.at[:, pl.ds(0, HALO)], ext.at[:, pl.ds(HALO + pan, HALO)], down),
    ]
    ahalo = [
        halo(2, vel.at[:, na - 1], velx.at[:, 0], (ax_up, az)),
        halo(3, vel.at[:, 0], velx.at[:, na + 1], (ax_down, az)),
        halo(4, visc.at[na - 1], viscx.at[0], (ax_up, az)),
        halo(5, visc.at[0], viscx.at[na + 1], (ax_down, az)),
    ]
    for c in fhalo:
        c.start()

    big = jnp.floor((cell_col + 1.0) * (1.0 / 64.0))
    small = (cell_col + 1.0) - 64.0 * big
    at_rank = lax.broadcasted_iota(jnp.int32, (pan, LANES), 1).astype(f32) == rank_col
    owner = lax.broadcasted_iota(jnp.int32, (n, pan), 0).astype(f32) == peer
    owner = owner.astype(f32).astype(bf16)
    cells = (64.0 * dot(owner, jnp.where(at_rank, big, 0.0).astype(bf16))
             + dot(owner, jnp.where(at_rank, small, 0.0).astype(bf16)) - 1.0)
    for d in range(n):
        scell[d] = cells[d:d + 1, :]

    def split_force(lo_row, hi_row):
        h, l = split(ext[:, lo_row:hi_row])
        exthi[:, lo_row:hi_row] = h
        extlo[:, lo_row:hi_row] = l

    loads[0].wait()
    split_force(HALO, HALO + pan)
    for c in fhalo:
        c.wait()
    split_force(0, HALO)
    split_force(HALO + pan, pan + 2 * HALO)

    def tiles_to(g, i):
        there = lax.rem(spot + i, half_n)
        side = 1 - half if g < n_ax else half
        device = (lax.rem(ax + g % n_ax, n_ax), side * half_n + there)
        src, k = g * half_n + there, g * half_n + i
        if early <= g < n_ax:
            at = (g - early) * half_n + spot
            tile_at, cell_at = got.at[at], gcell.at[at]
        else:
            at = (g if g < early else g - n_ax + early) * half_n + spot
            tile_at, cell_at = tiles.at[at], tcell.at[at]
        return (remote(send.at[src], tile_at, tile_send.at[k], tile_recv.at[k], device),
                remote(scell.at[src], cell_at, cell_send.at[k], cell_recv.at[k], device))

    def each_tile(groups, act):
        for g in groups:
            def body(i, carry):
                for c in tiles_to(g, i):
                    act(c)
                return carry
            lax.fori_loop(1 if g == n_ax else 0, half_n, body, 0)

    for part in range(2):
        r = slice(part * (slots // 2), (part + 1) * (slots // 2))
        for c in range(ncomp):
            tile = (dot(pick[r], exthi[c]) + dot(pick[r], extlo[c])) * scale[r]
            send[part * (n // 2):(part + 1) * (n // 2), :, c * nr:(c + 1) * nr] = (
                tile.reshape(n // 2, cap, nr))
        each_tile(range(part * n_ax, (part + 1) * n_ax), lambda c: c.start())
        if part == 0:
            for c in ahalo:
                c.start()
    own_src, own_dst = n_ax * half_n + spot, early * half_n + spot
    own = [pltpu.make_async_copy(send.at[own_src], tiles.at[own_dst], own_sem.at[0]),
           pltpu.make_async_copy(scell.at[own_src], tcell.at[own_dst], own_sem.at[1])]
    for c in own:
        c.start()

    loads[1].wait()
    loads[2].wait()
    for c in range(ncomp):
        edges[0, c] = velx[c, 1:na + 1, 0, :]
        edges[1, c] = velx[c, 1:na + 1, nt - 1, :]
    edges[0, ncomp] = viscx[1:na + 1, 0, :]
    edges[1, ncomp] = viscx[1:na + 1, nt - 1, :]
    zhalo = [
        halo(6, edges.at[1], edge_in.at[0], (ax, az_up)),
        halo(7, edges.at[0], edge_in.at[1], (ax, az_down)),
    ]
    for c in zhalo:
        c.start()
    for c in ahalo + zhalo:
        c.wait()

    @pl.when(ax == 0)
    def _():
        velx[:, 0] = jnp.zeros((ncomp, nt, nr), f32)
        viscx[0] = jnp.zeros((nt, nr), f32)

    @pl.when(ax == n_ax - 1)
    def _():
        velx[:, na + 1] = jnp.zeros((ncomp, nt, nr), f32)
        viscx[na + 1] = jnp.zeros((nt, nr), f32)

    row_id = lax.broadcasted_iota(jnp.int32, (nt, nr), 0)
    lane_id = lax.broadcasted_iota(jnp.int32, (nt, nr), 1)

    def neighbours(x, low, high):
        left = jnp.where(row_id == 0, low, pltpu.roll(x, 1, 0))
        right = jnp.where(row_id == nt - 1, high, pltpu.roll(x, nt - 1, 0))
        inner = jnp.where(lane_id == 0, 0.0, pltpu.roll(x, 1, 1))
        outer = jnp.where(lane_id == nr - 1, 0.0, pltpu.roll(x, nr - 1, 1))
        return left, right, inner, outer

    def plane(i, carry):
        mu = viscx[i + 1]
        sides = neighbours(mu, edge_in[0, ncomp, pl.ds(i, 1), :], edge_in[1, ncomp, pl.ds(i, 1), :])
        faces = [mu + s for s in (viscx[i], viscx[i + 2]) + sides]
        for c in range(ncomp):
            f = velx[c, i + 1]
            near = neighbours(f, edge_in[0, c, pl.ds(i, 1), :], edge_in[1, c, pl.ds(i, 1), :])
            near = (velx[c, i], velx[c, i + 2]) + near
            total = faces[0] * (near[0] - f)
            for w, g in zip(faces[1:], near[1:]):
                total = total + w * (g - f)
            acc[c, i] = f + (0.5 * step_size) * total
        return carry

    lax.fori_loop(0, na, plane, 0)

    late = list(range(early, n_ax))
    for c in own:
        c.wait()
    each_tile([g for g in range(2 * n_ax) if g not in late], lambda c: c.wait())
    h, l = split(tiles[...].reshape(-1, ncomp * nr))
    thi[...] = h
    tlo[...] = l
    crow = wide_row(tcell[...].reshape(-1, LANES), cap)
    blk = max(1, 256 // nt)

    def stored(j):
        return pltpu.make_async_copy(acc.at[:, pl.ds(j * blk, blk)],
                                     base.at[:, pl.ds(j * blk, blk)], out_sem.at[j])

    for j in range(na // blk):
        landing = landing_of(crow, j * blk * nt, blk * nt)
        for c in range(ncomp):
            cs = slice(c * nr, (c + 1) * nr)
            deposit = dot(landing, thi[:, cs]) + dot(landing, tlo[:, cs])
            acc[c, j * blk:(j + 1) * blk] += deposit.reshape(blk, nt, nr)
        stored(j).start()
    for j in range(na // blk):
        stored(j).wait()
    each_tile(late, lambda c: c.wait())


def settle(cap, base, got, gcell, out, hi, lo, crow):
    step = pl.program_id(0)
    ncomp, blk, nt, nr = base.shape

    @pl.when(step == 0)
    def _():
        crow[...] = wide_row(gcell[...].reshape(-1, LANES), cap)
        h, l = split(got[...])
        hi[...] = h
        lo[...] = l

    landing = landing_of(crow[...], step * (blk * nt), blk * nt)
    for c in range(ncomp):
        cs = slice(c * nr, (c + 1) * nr)
        deposit = dot(landing, hi[:, cs]) + dot(landing, lo[:, cs])
        out[c] = base[c] + deposit.reshape(blk, nt, nr)


def on_device(n_ax, n_az, velocity, viscosity, force, area, adjacency, crossing, cell):
    n, half_n = n_ax * n_az, n_az // 2
    ncomp, pan, nr = force.shape
    na, nt = velocity.shape[1:3]
    cap = max(2, 2 * pan // n)
    cap = -(-cap // 8) * 8
    slots = n * cap
    late = (n_ax - n_ax // 2) * half_n
    soon = n - late
    f32, bf16 = jnp.float32, jnp.bfloat16
    any_ = pl.BlockSpec(memory_space=pl.ANY)
    vmem = pl.BlockSpec(memory_space=pltpu.VMEM)
    dma = pltpu.SemaphoreType.DMA
    base, got, gcell = pl.pallas_call(
        functools.partial(exchange, n_ax, n_az, cap),
        out_shape=(jax.ShapeDtypeStruct(velocity.shape, f32),
                   jax.ShapeDtypeStruct((late, cap, ncomp * nr), f32),
                   jax.ShapeDtypeStruct((late, 1, LANES), f32)),
        in_specs=[any_, any_, any_, vmem, vmem, vmem, vmem],
        out_specs=(any_, any_, any_),
        scratch_shapes=[
            pltpu.VMEM((ncomp, na + 2, nt, nr), f32),
            pltpu.VMEM((na + 2, nt, nr), f32),
            pltpu.VMEM((ncomp, pan + 2 * HALO, nr), f32),
            pltpu.VMEM((ncomp, pan + 2 * HALO, nr), bf16),
            pltpu.VMEM((ncomp, pan + 2 * HALO, nr), bf16),
            pltpu.VMEM((n, cap, ncomp * nr), f32),
            pltpu.VMEM((n, 1, LANES), f32),
            pltpu.VMEM((2, ncomp + 1, na, nr), f32),
            pltpu.VMEM((2, ncomp + 1, na, nr), f32),
            pltpu.VMEM((ncomp, na, nt, nr), f32),
            pltpu.VMEM((soon, cap, ncomp * nr), f32),
            pltpu.VMEM((soon, 1, LANES), f32),
            pltpu.VMEM((soon * cap, ncomp * nr), bf16),
            pltpu.VMEM((soon * cap, ncomp * nr), bf16),
            dma((3,)), dma((8,)), dma((8,)), dma((n,)), dma((n,)), dma((n,)), dma((n,)),
            dma((2,)), dma((na,)),
        ],
        compiler_params=pltpu.CompilerParams(collective_id=0, has_side_effects=True),
        name="exchange",
    )(velocity, viscosity, force, crossing.reshape(1, pan), cell.reshape(1, pan),
      area.reshape(1, pan), adjacency.T)
    blk = max(1, 128 // nt)
    window = pl.BlockSpec((ncomp, blk, nt, nr), lambda s: (0, s, 0, 0))
    return pl.pallas_call(
        functools.partial(settle, cap),
        out_shape=jax.ShapeDtypeStruct(velocity.shape, f32),
        grid=(na // blk,),
        in_specs=[window,
                  pl.BlockSpec((late * cap, ncomp * nr), lambda s: (0, 0)),
                  pl.BlockSpec((late, 1, LANES), lambda s: (0, 0, 0))],
        out_specs=window,
        scratch_shapes=[pltpu.VMEM((late * cap, ncomp * nr), bf16),
                        pltpu.VMEM((late * cap, ncomp * nr), bf16),
                        pltpu.VMEM((1, late * cap), f32)],
        name="settle",
    )(base, got.reshape(late * cap, ncomp * nr), gcell)


def solution(mesh):
    n_ax, n_az = mesh.shape["ax"], mesh.shape["az"]
    in_specs = (
        P(None, "ax", "az", None),
        P("ax", "az", None),
        P(None, ("ax", "az"), None),
        P(("ax", "az")),
        P(("ax", "az"), None),
        P(("ax", "az"), None),
        P(("ax", "az")),
    )
    return jax.shard_map(
        functools.partial(on_device, n_ax, n_az), mesh=mesh, in_specs=in_specs,
        out_specs=P(None, "ax", "az", None), check_vma=False)
```

```python
import functools

import jax
import jax.numpy as jnp
from jax import lax
from jax.experimental import pallas as pl
from jax.experimental.pallas import tpu as pltpu
from jax.sharding import PartitionSpec as P

HALO = 32
LANES = 128

step_size = 0.1
coupling = 0.2


def split(x):
    hi = x.astype(jnp.bfloat16)
    lo = (x - hi.astype(jnp.float32)).astype(jnp.bfloat16)
    return hi, lo


def dot(a, b):
    return jnp.dot(a, b, preferred_element_type=jnp.float32)


def wide_row(cells, cap):
    m = cells.shape[0]
    slots = m * cap
    big = jnp.floor((cells + 1.0) * (1.0 / 64.0))
    small = (cells + 1.0) - 64.0 * big
    spread = (lax.broadcasted_iota(jnp.int32, (LANES, slots), 0)
              == lax.rem(lax.broadcasted_iota(jnp.int32, (LANES, slots), 1), cap))
    spread = spread.astype(jnp.float32).astype(jnp.bfloat16)
    wide = 64.0 * dot(big.astype(jnp.bfloat16), spread) + dot(small.astype(jnp.bfloat16), spread)
    mine = (lax.broadcasted_iota(jnp.int32, (m, slots), 0)
            == lax.broadcasted_iota(jnp.int32, (m, slots), 1) // cap)
    return jnp.sum(jnp.where(mine, wide, 0.0), axis=0, keepdims=True) - 1.0


def landing_of(crow, first, count):
    here = lax.broadcasted_iota(jnp.int32, (count, crow.shape[1]), 0) + first
    return (crow.astype(jnp.int32) == here).astype(jnp.float32).astype(jnp.bfloat16)


def exchange(n_ax, n_az, cap, vel, visc, force, dest_i, cell_i, area, adj_i, base, got, gcell,
             velx, viscx, ext, exthi, extlo, send, scell, edges, edge_in, acc,
             tiles, tcell, thi, tlo,
             load_sem, halo_send, halo_recv, tile_send, tile_recv,
             cell_send, cell_recv, own_sem, out_sem):
    n, half_n = n_ax * n_az, n_az // 2
    early = n_ax // 2
    ax, az = lax.axis_index("ax"), lax.axis_index("az")
    me = ax * n_az + az
    half, spot = az // half_n, lax.rem(az, half_n)
    ncomp, na, nt, nr = vel.shape
    pan = force.shape[1]
    slots = n * cap
    f32, bf16 = jnp.float32, jnp.bfloat16

    def place(linear):
        return (linear // n_az, lax.rem(linear, n_az))

    def remote(src, dst, ssem, rsem, device):
        return pltpu.make_async_remote_copy(
            src_ref=src, dst_ref=dst, send_sem=ssem, recv_sem=rsem,
            device_id=device, device_id_type=pl.DeviceIdType.MESH)

    barrier = pltpu.get_barrier_semaphore()

    def greet(k, carry):
        pl.semaphore_signal(barrier, inc=1, device_id=place(lax.rem(me + k, n)),
                            device_id_type=pl.DeviceIdType.MESH)
        return carry

    lax.fori_loop(1, n, greet, 0)
    loads = [
        pltpu.make_async_copy(force, ext.at[:, pl.ds(HALO, pan)], load_sem.at[0]),
        pltpu.make_async_copy(vel, velx.at[:, pl.ds(1, na)], load_sem.at[1]),
        pltpu.make_async_copy(visc, viscx.at[pl.ds(1, na)], load_sem.at[2]),
    ]
    for c in loads:
        c.start()

    dest_row, cell_row = dest_i[...].astype(f32), cell_i[...].astype(f32)
    adj = (adj_i[...] - (me * pan - HALO)).astype(f32)
    rows = jnp.concatenate([dest_row, cell_row, adj, dest_row, dest_row], axis=0)
    cols = rows.T
    dest_col, cell_col = cols[:, 0:1], cols[:, 1:2]
    same = dest_col == dest_row
    r0 = lax.broadcasted_iota(jnp.int32, (pan, pan), 0)
    r1 = lax.broadcasted_iota(jnp.int32, (pan, pan), 1)
    rank_row = jnp.sum((same & (r0 < r1)).astype(f32), axis=0, keepdims=True)
    rank_col = jnp.sum((same & (r1 < r0)).astype(f32), axis=1, keepdims=True)
    dax = jnp.floor(dest_row * (1.0 / n_az))
    daz = dest_row - n_az * dax
    dhalf = jnp.floor(daz * (1.0 / half_n))
    turn = dax - ax.astype(f32)
    turn = jnp.where(turn < 0.0, turn + n_ax, turn)
    group = turn + jnp.where(dhalf == half.astype(f32), float(n_ax), 0.0)
    peer = group * half_n + (daz - half_n * dhalf)
    target = (peer * cap + rank_row).astype(jnp.int32)
    hits = lax.broadcasted_iota(jnp.int32, (slots, pan), 0) == target
    scale = jnp.sum(jnp.where(hits, coupling * area[...], 0.0), axis=1, keepdims=True)
    q = lax.broadcasted_iota(jnp.int32, (pan, pan + 2 * HALO), 1).astype(f32)
    p = lax.broadcasted_iota(jnp.int32, (pan, pan + 2 * HALO), 0).astype(f32)
    count = (q == p + HALO).astype(f32)
    for k in range(4):
        count = count + (q == cols[:, 2 + k:3 + k]).astype(f32)
    pick = dot(hits.astype(f32).astype(bf16), count.astype(bf16)).astype(bf16)

    loads[1].wait()
    loads[2].wait()
    for c in range(ncomp):
        edges[0, c] = velx[c, 1:na + 1, 0, :]
        edges[1, c] = velx[c, 1:na + 1, nt - 1, :]
    edges[0, ncomp] = viscx[1:na + 1, 0, :]
    edges[1, ncomp] = viscx[1:na + 1, nt - 1, :]

    pl.semaphore_wait(barrier, n - 1)

    up, down = place(lax.rem(me + 1, n)), place(lax.rem(me + n - 1, n))
    ax_up, ax_down = lax.rem(ax + 1, n_ax), lax.rem(ax + n_ax - 1, n_ax)
    az_up, az_down = lax.rem(az + 1, n_az), lax.rem(az + n_az - 1, n_az)

    def halo(i, src, dst, device):
        return remote(src, dst, halo_send.at[i], halo_recv.at[i], device)

    fhalo = [
        halo(0, force.at[:, pl.ds(pan - HALO, HALO)], ext.at[:, pl.ds(0, HALO)], up),
        halo(1, force.at[:, pl.ds(0, HALO)], ext.at[:, pl.ds(HALO + pan, HALO)], down),
    ]
    ahalo = [
        halo(2, vel.at[:, na - 1], velx.at[:, 0], (ax_up, az)),
        halo(3, vel.at[:, 0], velx.at[:, na + 1], (ax_down, az)),
        halo(4, visc.at[na - 1], viscx.at[0], (ax_up, az)),
        halo(5, visc.at[0], viscx.at[na + 1], (ax_down, az)),
    ]
    zhalo = [
        halo(6, edges.at[1], edge_in.at[0], (ax, az_up)),
        halo(7, edges.at[0], edge_in.at[1], (ax, az_down)),
    ]
    for c in fhalo + zhalo + ahalo:
        c.start()

    big = jnp.floor((cell_col + 1.0) * (1.0 / 64.0))
    small = (cell_col + 1.0) - 64.0 * big
    at_rank = lax.broadcasted_iota(jnp.int32, (pan, LANES), 1).astype(f32) == rank_col
    owner = lax.broadcasted_iota(jnp.int32, (n, pan), 0).astype(f32) == peer
    owner = owner.astype(f32).astype(bf16)
    cells = (64.0 * dot(owner, jnp.where(at_rank, big, 0.0).astype(bf16))
             + dot(owner, jnp.where(at_rank, small, 0.0).astype(bf16)) - 1.0)
    for d in range(n):
        scell[d] = cells[d:d + 1, :]

    def split_force(lo_row, hi_row):
        h, l = split(ext[:, lo_row:hi_row])
        exthi[:, lo_row:hi_row] = h
        extlo[:, lo_row:hi_row] = l

    loads[0].wait()
    split_force(HALO, HALO + pan)
    for c in fhalo:
        c.wait()
    split_force(0, HALO)
    split_force(HALO + pan, pan + 2 * HALO)

    def tiles_to(g, i):
        there = lax.rem(spot + i, half_n)
        side = 1 - half if g < n_ax else half
        device = (lax.rem(ax + g % n_ax, n_ax), side * half_n + there)
        src, k = g * half_n + there, g * half_n + i
        if early <= g < n_ax:
            at = (g - early) * half_n + spot
            tile_at, cell_at = got.at[at], gcell.at[at]
        else:
            at = (g if g < early else g - n_ax + early) * half_n + spot
            tile_at, cell_at = tiles.at[at], tcell.at[at]
        return (remote(send.at[src], tile_at, tile_send.at[k], tile_recv.at[k], device),
                remote(scell.at[src], cell_at, cell_send.at[k], cell_recv.at[k], device))

    def each_tile(groups, act):
        for g in groups:
            def body(i, carry):
                for c in tiles_to(g, i):
                    act(c)
                return carry
            lax.fori_loop(1 if g == n_ax else 0, half_n, body, 0)

    for part in range(2):
        r = slice(part * (slots // 2), (part + 1) * (slots // 2))
        for c in range(ncomp):
            tile = (dot(pick[r], exthi[c]) + dot(pick[r], extlo[c])) * scale[r]
            send[part * (n // 2):(part + 1) * (n // 2), :, c * nr:(c + 1) * nr] = (
                tile.reshape(n // 2, cap, nr))
        each_tile(range(part * n_ax, (part + 1) * n_ax), lambda c: c.start())
    own_src, own_dst = n_ax * half_n + spot, early * half_n + spot
    own = [pltpu.make_async_copy(send.at[own_src], tiles.at[own_dst], own_sem.at[0]),
           pltpu.make_async_copy(scell.at[own_src], tcell.at[own_dst], own_sem.at[1])]
    for c in own:
        c.start()

    for c in ahalo + zhalo:
        c.wait()

    @pl.when(ax == 0)
    def _():
        velx[:, 0] = jnp.zeros((ncomp, nt, nr), f32)
        viscx[0] = jnp.zeros((nt, nr), f32)

    @pl.when(ax == n_ax - 1)
    def _():
        velx[:, na + 1] = jnp.zeros((ncomp, nt, nr), f32)
        viscx[na + 1] = jnp.zeros((nt, nr), f32)

    row_id = lax.broadcasted_iota(jnp.int32, (nt, nr), 0)
    lane_id = lax.broadcasted_iota(jnp.int32, (nt, nr), 1)

    def neighbours(x, low, high):
        left = jnp.where(row_id == 0, low, pltpu.roll(x, 1, 0))
        right = jnp.where(row_id == nt - 1, high, pltpu.roll(x, nt - 1, 0))
        inner = jnp.where(lane_id == 0, 0.0, pltpu.roll(x, 1, 1))
        outer = jnp.where(lane_id == nr - 1, 0.0, pltpu.roll(x, nr - 1, 1))
        return left, right, inner, outer

    def plane(i, carry):
        mu = viscx[i + 1]
        sides = neighbours(mu, edge_in[0, ncomp, pl.ds(i, 1), :], edge_in[1, ncomp, pl.ds(i, 1), :])
        faces = [mu + s for s in (viscx[i], viscx[i + 2]) + sides]
        for c in range(ncomp):
            f = velx[c, i + 1]
            near = neighbours(f, edge_in[0, c, pl.ds(i, 1), :], edge_in[1, c, pl.ds(i, 1), :])
            near = (velx[c, i], velx[c, i + 2]) + near
            total = faces[0] * (near[0] - f)
            for w, g in zip(faces[1:], near[1:]):
                total = total + w * (g - f)
            acc[c, i] = f + (0.5 * step_size) * total
        return carry

    lax.fori_loop(0, na, plane, 0)

    late = list(range(early, n_ax))
    for c in own:
        c.wait()
    each_tile([g for g in range(2 * n_ax) if g not in late], lambda c: c.wait())
    h, l = split(tiles[...].reshape(-1, ncomp * nr))
    thi[...] = h
    tlo[...] = l
    crow = wide_row(tcell[...].reshape(-1, LANES), cap)
    blk = max(1, 256 // nt)

    def stored(j):
        return pltpu.make_async_copy(acc.at[:, pl.ds(j * blk, blk)],
                                     base.at[:, pl.ds(j * blk, blk)], out_sem.at[j])

    for j in range(na // blk):
        landing = landing_of(crow, j * blk * nt, blk * nt)
        for c in range(ncomp):
            cs = slice(c * nr, (c + 1) * nr)
            deposit = dot(landing, thi[:, cs]) + dot(landing, tlo[:, cs])
            acc[c, j * blk:(j + 1) * blk] += deposit.reshape(blk, nt, nr)
        stored(j).start()
    for j in range(na // blk):
        stored(j).wait()
    each_tile(late, lambda c: c.wait())


def settle(cap, base, got, gcell, out, hi, lo, crow):
    step = pl.program_id(0)
    ncomp, blk, nt, nr = base.shape

    @pl.when(step == 0)
    def _():
        crow[...] = wide_row(gcell[...].reshape(-1, LANES), cap)
        h, l = split(got[...])
        hi[...] = h
        lo[...] = l

    landing = landing_of(crow[...], step * (blk * nt), blk * nt)
    for c in range(ncomp):
        cs = slice(c * nr, (c + 1) * nr)
        deposit = dot(landing, hi[:, cs]) + dot(landing, lo[:, cs])
        out[c] = base[c] + deposit.reshape(blk, nt, nr)


def on_device(n_ax, n_az, velocity, viscosity, force, area, adjacency, crossing, cell):
    n, half_n = n_ax * n_az, n_az // 2
    ncomp, pan, nr = force.shape
    na, nt = velocity.shape[1:3]
    cap = max(2, 2 * pan // n)
    cap = -(-cap // 8) * 8
    slots = n * cap
    late = (n_ax - n_ax // 2) * half_n
    soon = n - late
    f32, bf16 = jnp.float32, jnp.bfloat16
    any_ = pl.BlockSpec(memory_space=pl.ANY)
    hbm = pl.BlockSpec(memory_space=pltpu.HBM)
    vmem = pl.BlockSpec(memory_space=pltpu.VMEM)
    dma = pltpu.SemaphoreType.DMA
    velocity, viscosity, force = (
        pltpu.with_memory_space_constraint(x, pltpu.HBM) for x in (velocity, viscosity, force))
    base, got, gcell = pl.pallas_call(
        functools.partial(exchange, n_ax, n_az, cap),
        out_shape=(jax.ShapeDtypeStruct(velocity.shape, f32),
                   jax.ShapeDtypeStruct((late, cap, ncomp * nr), f32),
                   jax.ShapeDtypeStruct((late, 1, LANES), f32)),
        in_specs=[hbm, hbm, hbm, vmem, vmem, vmem, vmem],
        out_specs=(any_, any_, any_),
        scratch_shapes=[
            pltpu.VMEM((ncomp, na + 2, nt, nr), f32),
            pltpu.VMEM((na + 2, nt, nr), f32),
            pltpu.VMEM((ncomp, pan + 2 * HALO, nr), f32),
            pltpu.VMEM((ncomp, pan + 2 * HALO, nr), bf16),
            pltpu.VMEM((ncomp, pan + 2 * HALO, nr), bf16),
            pltpu.VMEM((n, cap, ncomp * nr), f32),
            pltpu.VMEM((n, 1, LANES), f32),
            pltpu.VMEM((2, ncomp + 1, na, nr), f32),
            pltpu.VMEM((2, ncomp + 1, na, nr), f32),
            pltpu.VMEM((ncomp, na, nt, nr), f32),
            pltpu.VMEM((soon, cap, ncomp * nr), f32),
            pltpu.VMEM((soon, 1, LANES), f32),
            pltpu.VMEM((soon * cap, ncomp * nr), bf16),
            pltpu.VMEM((soon * cap, ncomp * nr), bf16),
            dma((3,)), dma((8,)), dma((8,)), dma((n,)), dma((n,)), dma((n,)), dma((n,)),
            dma((2,)), dma((na,)),
        ],
        compiler_params=pltpu.CompilerParams(collective_id=0, has_side_effects=True,
                                             vmem_limit_bytes=40 << 20),
        name="exchange",
    )(velocity, viscosity, force, crossing.reshape(1, pan), cell.reshape(1, pan),
      area.reshape(1, pan), adjacency.T)
    blk = max(1, 128 // nt)
    window = pl.BlockSpec((ncomp, blk, nt, nr), lambda s: (0, s, 0, 0))
    return pl.pallas_call(
        functools.partial(settle, cap),
        out_shape=jax.ShapeDtypeStruct(velocity.shape, f32),
        grid=(na // blk,),
        in_specs=[window,
                  pl.BlockSpec((late * cap, ncomp * nr), lambda s: (0, 0)),
                  pl.BlockSpec((late, 1, LANES), lambda s: (0, 0, 0))],
        out_specs=window,
        scratch_shapes=[pltpu.VMEM((late * cap, ncomp * nr), bf16),
                        pltpu.VMEM((late * cap, ncomp * nr), bf16),
                        pltpu.VMEM((1, late * cap), f32)],
        compiler_params=pltpu.CompilerParams(vmem_limit_bytes=16 << 20),
        name="settle",
    )(base, got.reshape(late * cap, ncomp * nr), gcell)


def solution(mesh):
    n_ax, n_az = mesh.shape["ax"], mesh.shape["az"]
    in_specs = (
        P(None, "ax", "az", None),
        P("ax", "az", None),
        P(None, ("ax", "az"), None),
        P(("ax", "az")),
        P(("ax", "az"), None),
        P(("ax", "az"), None),
        P(("ax", "az")),
    )
    return jax.shard_map(
        functools.partial(on_device, n_ax, n_az), mesh=mesh, in_specs=in_specs,
        out_specs=P(None, "ax", "az", None), check_vma=False)
```
